256 devices in a mesh: expert: 8 (over y, x_lo), dp: 32 (over x_hi, z, core).
Axes of the slice: x: 4 (x_hi: 2, x_lo: 2; x = x_hi * 2 + x_lo), y: 4, z: 8, core: 2. Of those that a mesh axis runs over, the one named last changes fastest.
Arguments:
- tokens: bfloat16 [32768, 2048], P(('expert', 'dp')), may hold values from -6 to 6
- cotangent: bfloat16 [32768, 2048], P(('expert', 'dp')), may hold values from -3 to 3
- w_in: bfloat16 [8, 2048, 768], P('expert', 'dp'), may hold values from -0.125 to 0.125
- w_out: bfloat16 [8, 2048, 384], P('expert', 'dp'), may hold values from -0.3125 to 0.3125
- block_rows: int32 [256, 4, 64], P(('expert', 'dp')), may hold values from -1 to 127, as said below
- block_gates: float32 [256, 4, 64], P(('expert', 'dp')), may hold values from 0.1 to 1
- block_count: int32 [256, 2], P(('expert', 'dp')), may hold values from 1 to 2, as said below
Outputs:
- mixed: bfloat16 [32768, 2048], P(('expert', 'dp'))
- token_grad: bfloat16 [32768, 2048], P(('expert', 'dp'))
- gate_grad: float32 [256, 4, 64], P(('expert', 'dp'))
- grad_in: bfloat16 [8, 2048, 768], P('expert', 'dp')
- grad_out: bfloat16 [8, 2048, 384], P('expert', 'dp')
The draws below stay inside these ranges and needn't reach their ends.
Inputs may be any that keep to these rules, and one draw needn't show every extreme that they name: `block_rows`: for each shard and stop, the first block_count blocks list the tokens routed to that stop's expert in increasing order, followed by -1 entries to the end of the last used block; blocks beyond block_count hold arbitrary tokens of the shard. In every shard one stop receives all 128 tokens; each other stop receives a share of them that differs from shard to shard. `block_count`: the number of used blocks of each stop: the stop's routed tokens divided by 64, rounded up.
All inputs are finite; a program needn't handle non-finite values.
Results may differ from the reference program's by a relative error of at most 0.019.
Values may be sent and summed in bfloat16 or wider, within the bound.
No kernel may reach another device: no remote copies, remote signals or barrier semaphores. Data moves between devices by JAX's collectives and lax.ppermute only.
A program may use at most 64 MiB of HBM per device.

```python
import jax
import jax.numpy as jnp
from jax import lax

D = 2048
FFW = 384
BLOCK = 64
STOPS = 2
TOK_DEV = 128
MAXB = 2
SLOTS = 4
SHARDS = 256
TOKENS = 32768
EXPERTS = 8
N_DP = 32


def plan_rows(key):
    base_key = jax.random.fold_in(key, 4711)
    key_full, key_other, key_share = jax.random.split(base_key, 3)
    full_stop = jax.random.randint(key_full, (SHARDS,), 0, STOPS).astype(jnp.int32)
    share_cut = jax.random.randint(key_share, (SHARDS,), TOK_DEV // 5, 4 * TOK_DEV // 5 + 1).astype(jnp.int32)
    coin_vals = jax.random.randint(key_other, (SHARDS, TOK_DEV), 0, TOK_DEV).astype(jnp.int32)
    other_pick = coin_vals < share_cut[:, None]
    stop_ids = jnp.arange(STOPS, dtype=jnp.int32)
    is_full = stop_ids[None, :] == full_stop[:, None]
    chosen = is_full[:, :, None] | other_pick[:, None, :]
    filled = jnp.sum(chosen.astype(jnp.int32), axis=-1)
    positions = jnp.arange(TOK_DEV, dtype=jnp.int32)
    sort_keys = jnp.where(chosen, positions, TOK_DEV + positions)
    ordered = jnp.argsort(sort_keys, axis=-1, stable=True).astype(jnp.int32)
    blocks_used = ((filled + BLOCK - 1) // BLOCK).astype(jnp.int32)
    padded = jnp.where(positions < blocks_used[..., None] * BLOCK, -1, ordered)
    entries = jnp.where(positions < filled[..., None], ordered, padded)
    return (entries.reshape(SHARDS, SLOTS, BLOCK).astype(jnp.int32), blocks_used)


def draw_block_rows(key, part):
    return plan_rows(key)[0]


def draw_block_count(key, part):
    return plan_rows(key)[1]


def levels(own_key, extent, cuts, smallest, high):
    def one(dim, blocks):
        steps = jax.random.uniform(jax.random.fold_in(jax.random.fold_in(own_key, 6), dim), (blocks,), jnp.float32, smallest / len(cuts), high / len(cuts))
        return jnp.repeat(jnp.exp(steps), extent[dim] // blocks).reshape((-1,) + (1,) * (len(extent) - dim - 1))

    factor_of = one(*cuts[0])
    for cut in cuts[1:]:
        factor_of = factor_of * one(*cut)
    return factor_of


def bell_draw(key, extent, scale, bound, cuts=(), held_as=jnp.bfloat16):
    values = scale * jax.random.normal(key, extent, jnp.float32)
    if cuts:
        values = values * levels(key, extent, cuts, -0.22, 0.18)
    return jnp.clip(values, -bound, bound).astype(held_as)


def setup_inputs(seed: int = 0) -> dict:
    splits = jax.random.split(jax.random.key(seed), 8)
    return {
        "tokens": bell_draw(splits[0], (TOKENS, D), 1.0, 6.0, ((0, 256),)),
        "cotangent": bell_draw(splits[1], (TOKENS, D), 0.5, 3.0, ((0, 256),)),
        "w_in": bell_draw(splits[2], (EXPERTS, D, 2 * FFW), D ** -0.5, 0.125, ((0, 8), (1, 32))),
        "w_out": bell_draw(splits[3], (EXPERTS, D, FFW), FFW ** -0.5, 0.3125, ((0, 8), (1, 32))),
        "block_rows": draw_block_rows(jax.random.fold_in(splits[7], 71), 0),
        "block_gates": jnp.clip(0.1 + 0.9 * jax.random.uniform(splits[5], (SHARDS, SLOTS, BLOCK), jnp.float32) ** levels(splits[5], (SHARDS, SLOTS, BLOCK), ((0, 256),), -0.2, 0.2), 0.1, 1.0),
        "block_count": draw_block_count(jax.random.fold_in(splits[7], 71), 0),
    }


def silu_pair(preact):
    sigmoid_val = jax.nn.sigmoid(preact)
    return preact * sigmoid_val, sigmoid_val * (1.0 + preact * (1.0 - sigmoid_val))


def contract_rows(left_mat, right_mat):
    return lax.dot_general(left_mat, right_mat, (((0,), (0,)), ((), ())), preferred_element_type=jnp.float32)


def contract_cols(left_mat, right_mat):
    return lax.dot_general(left_mat, right_mat, (((1,), (1,)), ((), ())), preferred_element_type=jnp.float32)


def expert_pass(inputs, gated_cot, slab_in, slab_out):
    hidden_width = slab_out.shape[1]
    preact = jnp.dot(inputs, slab_in, preferred_element_type=jnp.float32)
    gate_pre = preact[:, :hidden_width]
    up_pre = preact[:, hidden_width:]
    activated, derivative = silu_pair(gate_pre)
    hidden = (activated * up_pre).astype(jnp.bfloat16)
    output = contract_cols(hidden, slab_out)
    act_grad = jnp.dot(gated_cot, slab_out, preferred_element_type=jnp.float32)
    hid_grad = jnp.concatenate([act_grad * up_pre * derivative, act_grad * activated], axis=1).astype(jnp.bfloat16)
    input_grad = contract_cols(hid_grad, slab_in)
    return output, input_grad, hidden, hid_grad


def slot_masks(entries, gate_vals, block_total):
    positions = jnp.arange(entries.shape[0], dtype=jnp.int32)
    live_mask = ((positions // BLOCK < block_total) & (entries >= 0)).astype(jnp.float32)
    token_ids = jnp.where(entries >= 0, entries, 0).astype(jnp.int32)
    return live_mask, token_ids, gate_vals * live_mask


def reference(tokens, cotangent, w_in, w_out, block_rows, block_gates, block_count):
    slot_span = MAXB * BLOCK
    token_blocks = tokens.reshape(SHARDS, TOK_DEV, D)
    cot_blocks = cotangent.reshape(SHARDS, TOK_DEV, D)
    row_blocks = block_rows.reshape(SHARDS, STOPS, slot_span)
    gate_blocks = block_gates.reshape(SHARDS, STOPS, slot_span)

    def one_shard(running, packed):
        sum_in, sum_out = running
        shard_id, inputs_all, cot_block, row_table, gate_table, block_total = packed
        cycle_pos = shard_id // N_DP
        mixed_sum = jnp.zeros((TOK_DEV, D), jnp.float32)
        token_sum = jnp.zeros((TOK_DEV, D), jnp.float32)
        gate_list = []
        for station in range(STOPS):
            expert = ((cycle_pos - station) % EXPERTS).astype(jnp.int32)
            live_mask, token_ids, weight = slot_masks(row_table[station], gate_table[station], block_total[station])
            inputs = inputs_all[token_ids]
            cot_rows = cot_block[token_ids]
            gated_cot = (weight[:, None] * cot_rows.astype(jnp.float32)).astype(jnp.bfloat16)
            output, input_grad, hidden, hid_grad = expert_pass(inputs, gated_cot, w_in[expert], w_out[expert])
            mixed_sum = mixed_sum.at[token_ids].add(weight[:, None] * output)
            token_sum = token_sum.at[token_ids].add(input_grad)
            gate_list.append(live_mask * jnp.sum(output * cot_rows.astype(jnp.float32), axis=1))
            term_in = contract_rows(inputs, hid_grad).astype(jnp.bfloat16)
            term_out = contract_rows(gated_cot, hidden).astype(jnp.bfloat16)
            term_in, term_out = lax.optimization_barrier((term_in, term_out))
            sum_in = sum_in.at[expert].add(term_in.astype(jnp.float32))
            sum_out = sum_out.at[expert].add(term_out.astype(jnp.float32))
        outputs = (mixed_sum.astype(jnp.bfloat16), token_sum.astype(jnp.bfloat16), jnp.stack(gate_list))
        return (sum_in, sum_out), outputs

    initial = (jnp.zeros((EXPERTS, D, 2 * FFW), jnp.float32), jnp.zeros((EXPERTS, D, FFW), jnp.float32))
    shard_ids = jnp.arange(SHARDS, dtype=jnp.int32)
    totals, results = lax.scan(one_shard, initial, (shard_ids, token_blocks, cot_blocks, row_blocks, gate_blocks, block_count))
    mixed = results[0].reshape(TOKENS, D)
    token_grad = results[1].reshape(TOKENS, D)
    gate_grad = results[2].reshape(SHARDS, SLOTS, BLOCK)
    return mixed, token_grad, gate_grad, totals[0].astype(jnp.bfloat16), totals[1].astype(jnp.bfloat16)
```

```python
import jax
import jax.numpy as jnp
from jax import lax
from jax.sharding import Mesh
from jax.sharding import PartitionSpec as P

DP = ("dp_0", "dp_1", "dp_2")
EXPERT_DP = ("expert", "dp_0", "dp_1", "dp_2")
ZC = ("dp_1", "dp_2")
F32 = jnp.float32
BF16 = jnp.bfloat16


def around(value, axis, distance):
    n = lax.axis_size(axis)
    return lax.ppermute(value, axis, [(i, (i + distance) % n) for i in range(n)])


def onward(value):
    n = lax.axis_size("dp_1")
    route = [(z * 2 + c, (z + 1 - 2 * c) % n * 2 + c) for z in range(n) for c in range(2)]
    return lax.ppermute(value, ZC, route)


def twin(value):
    return lax.ppermute(value, "dp_2", [(0, 1), (1, 0)])


def across(value):
    return lax.ppermute(value, "dp_0", [(0, 1), (1, 0)])


def rows_dot(left, right):
    return lax.dot_general(left, right, (((0,), (0,)), ((), ())), preferred_element_type=F32)


def cols_dot(left, right):
    return lax.dot_general(left, right, (((1,), (1,)), ((), ())), preferred_element_type=F32)


def body(tokens, cotangent, w_in, w_out, block_rows, block_gates, block_count):
    count, width = tokens.shape
    stops = block_count.shape[1]
    block = block_rows.shape[2]
    slots = block_rows.shape[1] // stops * block
    rows, hidden = w_out.shape[1:]
    pair = 2 * rows
    ring = lax.axis_size("dp_1")
    half = ring // 2
    here_x, here_z, core = (lax.axis_index(name) for name in DP)
    first = core == 0
    sign = 2 * core - 1

    def in_order(mine, other):
        return jnp.where(first, jnp.concatenate([mine, other]), jnp.concatenate([other, mine]))

    entries = block_rows.reshape(stops, slots)
    place = jnp.arange(slots, dtype=jnp.int32) // block
    live = (place[None] < block_count[0][:, None]) & (entries >= 0)
    named = (entries[:, :, None] == jnp.arange(count, dtype=jnp.int32)) & live[:, :, None]
    gates = jnp.sum(jnp.where(named, block_gates.reshape(stops, slots)[:, :, None], 0.0), axis=1)

    shard = jnp.concatenate([w_in[0], w_out[0]], axis=1)
    far_shard = across(shard)
    own_chain = [in_order(shard, twin(shard))]
    far_tokens = around(tokens, "expert", -1)
    far_cot = around(cotangent, "expert", -1)
    far_gates = around(gates[1:2], "expert", -1)
    far_chain = [in_order(far_shard, twin(far_shard))]
    for k in range(1, half):
        for chain in (own_chain, far_chain):
            chain.append(onward(chain[-1]))
    chains = []
    for chain in (own_chain, far_chain):
        last = onward(lax.dynamic_slice_in_dim(chain[-1], core * rows, rows, 0))
        back = [twin(piece) for piece in chain[1:]]
        chains += chain + [in_order(last, twin(last))] + back[::-1]
    slab = jnp.concatenate(chains)
    slab_in, slab_out = slab[:, : 2 * hidden], slab[:, 2 * hidden :]

    def column(value, p, q):
        at = ((here_x + p) % 2 * ring + (here_z + sign * q) % ring) * pair
        return lax.dynamic_slice_in_dim(value, at, pair, 1)

    def turned(value):
        return jnp.concatenate([column(value, p, q) for p in range(2) for q in range(ring)], axis=1)

    def turned_back(value):
        pieces = []
        for x in range(2):
            for z in range(ring):
                at = ((here_x + x) % 2 * ring + sign * (z - here_z) % ring) * pair
                pieces.append(lax.dynamic_slice_in_dim(value, at, pair, 1))
        return jnp.concatenate(pieces, axis=1)

    inputs = jnp.concatenate([tokens, far_tokens])
    cots = jnp.concatenate([cotangent, far_cot])
    gate = jnp.concatenate([gates[0], far_gates[0]])[:, None]
    preact = jnp.dot(turned(inputs), slab_in, preferred_element_type=F32)
    plain = jnp.dot(turned(cots), slab_out, preferred_element_type=F32)
    gate_pre, up_pre = preact[:, :hidden], preact[:, hidden:]
    sig = jax.nn.sigmoid(gate_pre)
    activated = gate_pre * sig
    derivative = sig * (1.0 + gate_pre * (1.0 - sig))
    act = activated * up_pre
    act_grad = gate * plain
    gated = (gate * act).astype(BF16)
    hid_grad = jnp.concatenate(
        [act_grad * up_pre * derivative, act_grad * activated], axis=1
    ).astype(BF16)
    score = jnp.sum(act * plain, axis=1)

    back_mixed = around(turned_back(cols_dot(gated[count:], slab_out).astype(BF16)), "expert", 1)
    back_grad = around(turned_back(cols_dot(hid_grad[count:], slab_in).astype(BF16)), "expert", 1)
    back_score = around(score[None, count:], "expert", 1)

    all_inputs = jnp.concatenate([inputs, twin(tokens), twin(far_tokens)])
    all_cots = jnp.concatenate([cots, twin(cotangent), twin(far_cot)])
    all_hid = jnp.concatenate([hid_grad, twin(hid_grad)])
    all_gated = jnp.concatenate([gated, twin(gated)])

    def term(p, q):
        return jnp.concatenate(
            [
                rows_dot(column(all_inputs, p, q), all_hid),
                rows_dot(column(all_cots, p, q), all_gated),
            ],
            axis=1,
        )

    def own_rows(value):
        return lax.dynamic_slice_in_dim(value, core * rows, rows, 0)

    def other_rows(value):
        return lax.dynamic_slice_in_dim(value, (1 - core) * rows, rows, 0)

    sums = [None, None]
    passed = [None, None]
    for p in (1, 0):
        passed[p] = onward(own_rows(term(p, half)).astype(BF16))
    mine = jnp.arange(pair)[:, None] // rows == core
    for k in range(half - 1, 0, -1):
        for p in (1, 0):
            come = passed[p].astype(F32)
            if k == half - 1:
                come = jnp.where(mine, jnp.concatenate([come, come]), 0.0)
            passed[p] = onward((term(p, ring - k) + come).astype(BF16))
    for p in (1, 0):
        kept = own_rows(passed[p]).astype(F32) + own_rows(term(p, 0))
        sums[p] = kept + twin(other_rows(passed[p])).astype(F32)
    total = sums[0] + across(sums[1].astype(BF16)).astype(F32)

    mixed = turned_back(cols_dot(gated[:count], slab_out)) + back_mixed.astype(F32)
    token_grad = turned_back(cols_dot(hid_grad[:count], slab_in)) + back_grad.astype(F32)
    scores = jnp.concatenate([score[None, :count], back_score])
    gate_grad = jnp.sum(jnp.where(named, scores[:, None, :], 0.0), axis=2)
    total = total.astype(BF16)
    return (
        mixed.astype(BF16),
        token_grad.astype(BF16),
        gate_grad.reshape(block_gates.shape),
        total[None, :, : 2 * hidden],
        total[None, :, 2 * hidden :],
    )


def solution(mesh):
    split = Mesh(
        mesh.devices.reshape(mesh.shape["expert"], 2, 8, 2), ("expert", "dp_0", "dp_1", "dp_2")
    )
    in_specs = (
        P(EXPERT_DP, None),
        P(EXPERT_DP, None),
        P("expert", DP, None),
        P("expert", DP, None),
        P(EXPERT_DP, None, None),
        P(EXPERT_DP, None, None),
        P(EXPERT_DP, None),
    )
    out_specs = (
        P(EXPERT_DP, None),
        P(EXPERT_DP, None),
        P(EXPERT_DP, None, None),
        P("expert", DP, None),
        P("expert", DP, None),
    )
    return jax.shard_map(body, mesh=split, in_specs=in_specs, out_specs=out_specs, check_vma=False)
```

```python
import jax
import jax.numpy as jnp
from jax import lax
from jax.experimental import pallas as pl
from jax.experimental.pallas import tpu as pltpu
from jax.sharding import Mesh
from jax.sharding import PartitionSpec as P

DP = ("dp_0", "dp_1", "dp_2")
EXPERT_DP = ("expert", "dp_0", "dp_1", "dp_2")
ZC = ("dp_1", "dp_2")
F32 = jnp.float32
BF16 = jnp.bfloat16


def around(value, distance):
    n = lax.axis_size("expert")
    return lax.ppermute(value, "expert", [(i, (i + distance) % n) for i in range(n)])


def onward(value):
    n = lax.axis_size("dp_1")
    route = [(z * 2 + c, (z + 1 - 2 * c) % n * 2 + c) for z in range(n) for c in range(2)]
    return lax.ppermute(value, ZC, route)


def twin(value):
    return lax.ppermute(value, "dp_2", [(0, 1), (1, 0)])


def across(value):
    return lax.ppermute(value, "dp_0", [(0, 1), (1, 0)])


def cols_dot(left, right):
    return lax.dot_general(left, right, (((1,), (1,)), ((), ())), preferred_element_type=F32)


def column_start(here, p, q, ring, pair):
    at = ((here[0] + p) % 2 * ring + (here[1] + here[2] * q + ring) % ring) * pair
    return pl.multiple_of(at, pair)


def kernel_call(kernel, out_shape, operands, scratch=(), room=12):
    vmem = pl.BlockSpec(memory_space=pltpu.VMEM)
    held = [pltpu.with_memory_space_constraint(x, pltpu.VMEM) for x in operands[1:]]
    return pl.pallas_call(
        kernel,
        out_shape=out_shape,
        in_specs=[pl.BlockSpec(memory_space=pltpu.SMEM)] + [vmem] * len(held),
        out_specs=tuple(vmem for _ in out_shape),
        scratch_shapes=scratch,
        compiler_params=pltpu.CompilerParams(vmem_limit_bytes=room << 20),
    )(operands[0], *held)


def named_tokens(rows_ref, counts_ref, block, stops, count):
    each = rows_ref.shape[0] // stops
    entries = rows_ref[block : block + 1, :]
    token = lax.broadcasted_iota(jnp.int32, (count, entries.shape[1]), 0)
    return (entries == token) & (block % each < counts_ref[0, block // each])


def prepare(tokens, cotangent, block_rows, block_gates, block_count):
    count, width = tokens.shape
    blocks = block_rows.shape[0]
    stops = block_count.shape[1]
    each = blocks // stops

    def kernel(counts_ref, rows_ref, gates_ref, tokens_ref, cot_ref, both_ref, *refs):
        *out_refs, sems = refs
        copies = [
            pltpu.make_async_copy(tokens_ref, both_ref.at[:count, :], sems.at[0]),
            pltpu.make_async_copy(cot_ref, both_ref.at[count:, :], sems.at[1]),
        ]
        for copy in copies:
            copy.start()
        for stop in range(stops):
            total = jnp.zeros((count, 1), F32)
            for block in range(stop * each, (stop + 1) * each):
                named = named_tokens(rows_ref, counts_ref, block, stops, count)
                gates = jnp.where(named, gates_ref[block : block + 1, :], 0.0)
                total += jnp.sum(gates, axis=1, keepdims=True)
            out_refs[stop][...] = total
        for copy in copies:
            copy.wait()

    vmem = pl.BlockSpec(memory_space=pltpu.VMEM)
    anywhere = pl.BlockSpec(memory_space=pl.ANY)
    shapes = (pltpu.VMEM((2 * count, width), BF16),) + (pltpu.VMEM((count, 1), F32),) * stops
    return pl.pallas_call(
        kernel,
        out_shape=shapes,
        in_specs=[pl.BlockSpec(memory_space=pltpu.SMEM), vmem, vmem, anywhere, anywhere],
        out_specs=tuple(vmem for _ in shapes),
        scratch_shapes=[pltpu.SemaphoreType.DMA((2,))],
        compiler_params=pltpu.CompilerParams(vmem_limit_bytes=4 << 20),
    )(block_count, block_rows, block_gates, tokens, cotangent)


def turn_columns(here, mine, other, ring, pair):
    both, width = mine.shape
    count = both // 2

    def kernel(here_ref, mine_ref, other_ref, turned_ref, *flat_refs):
        spot = [here_ref[i] for i in range(3)]
        for p in range(2):
            for q in range(ring):
                at = column_start(spot, p, q, ring, pair)
                to = (p * ring + q) * pair
                own = mine_ref[:, pl.ds(at, pair)]
                turned_ref[:, to : to + pair] = own
                if q >= ring // 2 or q == 0:
                    twins = other_ref[:, pl.ds(at, pair)]
                    for i in range(2):
                        rows = slice(i * count, (i + 1) * count)
                        flat_refs[i][to : to + pair, :count] = own[rows].T
                        flat_refs[i][to : to + pair, count:] = twins[rows].T

    shapes = (
        pltpu.VMEM((both, width), BF16),
        pltpu.VMEM((width, both), BF16),
        pltpu.VMEM((width, both), BF16),
    )
    return kernel_call(kernel, shapes, (here, mine, other))


def hidden_values(here, near, far, gates, pieces, pair, hidden):
    both, width = near.shape
    count = both // 2
    keep = pair // 2
    arrays = list({id(piece[0]): piece[0] for piece in pieces}.values())
    index = {id(array): i for i, array in enumerate(arrays)}
    plan = [(index[id(piece[0])], *piece[1:]) for piece in pieces]

    def kernel(here_ref, near_ref, far_ref, near_gate_ref, far_gate_ref, *refs):
        piece_refs = refs[: len(arrays)]
        slab_ref, act_ref, near_score_ref, far_score_ref, in_ref, cot_ref = refs[len(arrays) :]
        core = here_ref[3]
        for which, take, to, twins in plan:
            at = to + keep * (1 - core if twins else core)
            slab_ref[pl.ds(pl.multiple_of(at, keep), keep), :] = piece_refs[which][take, :]
        in_ref[:count, :] = near_ref[:count, :]
        in_ref[count:, :] = far_ref[:count, :]
        cot_ref[:count, :] = near_ref[count:, :]
        cot_ref[count:, :] = far_ref[count:, :]
        slab_in = slab_ref[:, : 2 * hidden]
        preact = jnp.dot(in_ref[...], slab_in, preferred_element_type=F32)
        plain = jnp.dot(cot_ref[...], slab_ref[:, 2 * hidden :], preferred_element_type=F32)
        gate_pre, up_pre = preact[:, :hidden], preact[:, hidden:]
        gate = jnp.concatenate([near_gate_ref[...], far_gate_ref[...]])
        sig = jax.nn.sigmoid(gate_pre)
        activated = gate_pre * sig
        derivative = sig * (1.0 + gate_pre * (1.0 - sig))
        act = activated * up_pre
        act_grad = gate * plain
        act_ref[:, :hidden] = (act_grad * up_pre * derivative).astype(BF16)
        act_ref[:, hidden : 2 * hidden] = (act_grad * activated).astype(BF16)
        act_ref[:, 2 * hidden :] = (gate * act).astype(BF16)
        score = jnp.sum(act * plain, axis=1, keepdims=True)
        near_score_ref[...] = score[:count]
        far_score_ref[...] = score[count:]

    shapes = (
        pltpu.VMEM((width, 3 * hidden), BF16),
        pltpu.VMEM((both, 3 * hidden), BF16),
        pltpu.VMEM((count, 1), F32),
        pltpu.VMEM((count, 1), F32),
    )
    scratch = [pltpu.VMEM((both, width), BF16)] * 2
    return kernel_call(kernel, shapes, (here, near, far, *gates, *arrays), scratch)


def token_values(here, act, slab, ring, pair, hidden):
    width = slab.shape[0]
    count = act.shape[0] // 2

    def kernel(here_ref, act_ref, slab_ref, far_ref, near_ref):
        spot = [here_ref[i] for i in range(3)]
        values = (
            cols_dot(act_ref[:, 2 * hidden :], slab_ref[:, 2 * hidden :]),
            cols_dot(act_ref[:, : 2 * hidden], slab_ref[:, : 2 * hidden]),
        )
        for p in range(2):
            for q in range(ring):
                at = column_start(spot, p, q, ring, pair)
                came = (p * ring + q) * pair
                for i in range(2):
                    rows = slice(i * count, (i + 1) * count)
                    piece = values[i][:, came : came + pair]
                    near_ref[rows, pl.ds(at, pair)] = piece[:count]
                    far_ref[rows, pl.ds(at, pair)] = piece[count:].astype(BF16)

    shapes = (pltpu.VMEM((2 * count, width), BF16), pltpu.VMEM((2 * count, width), F32))
    return kernel_call(kernel, shapes, (here, act, slab))


def finish_tokens(block_count, near, come, scores, block_rows):
    both, width = near.shape
    count = both // 2
    stops = block_count.shape[1]
    each = block_rows.shape[0] // stops

    def kernel(counts_ref, near_ref, come_ref, *refs):
        score_refs, (rows_ref, mixed_ref, grad_ref, gates_ref) = refs[:stops], refs[stops:]
        mixed_ref[...] = (near_ref[:count, :] + come_ref[:count, :].astype(F32)).astype(BF16)
        grad_ref[...] = (near_ref[count:, :] + come_ref[count:, :].astype(F32)).astype(BF16)
        for block in range(stops * each):
            named = named_tokens(rows_ref, counts_ref, block, stops, count)
            picked = jnp.where(named, score_refs[block // each][...], 0.0)
            gates_ref[block : block + 1, :] = jnp.sum(picked, axis=0, keepdims=True)

    shape = jax.ShapeDtypeStruct((count, width), BF16)
    shapes = (shape, shape, jax.ShapeDtypeStruct(block_rows.shape, F32))
    return kernel_call(kernel, shapes, (block_count, near, come, *scores, block_rows))


def all_acts(act_ref, twin_ref, all_ref):
    count = act_ref.shape[0] // 2
    for i in range(2):
        rows = slice(i * count, (i + 1) * count)
        all_ref[2 * i * count : (2 * i + 1) * count, :] = act_ref[rows, :]
        all_ref[(2 * i + 1) * count : (2 * i + 2) * count, :] = twin_ref[rows, :]


def weight_terms(here, flats, act, act_twin, wanted, ring, pair, hidden):
    keep = pair // 2
    both = act.shape[0]
    groups = [group for _, parts in wanted for group in parts]

    def kernel(here_ref, *refs):
        flat_refs, (act_ref, twin_ref), out_refs = refs[:4], refs[4:6], refs[6:-2]
        left_ref, all_ref = refs[-2:]
        all_acts(act_ref, twin_ref, all_ref)
        core = here_ref[3]
        for i, cut in ((0, slice(0, 2 * hidden)), (1, slice(2 * hidden, 3 * hidden))):
            for g, (p, q, twins) in enumerate(groups):
                at = (p * ring + q) * pair + keep * (1 - core if twins else core)
                rows = pl.ds(pl.multiple_of(at, keep), keep)
                for j in range(2):
                    left_ref[i, g * keep : (g + 1) * keep, j * both : (j + 1) * both] = flat_refs[
                        2 * j + i
                    ][rows, :]
            total = jnp.dot(left_ref[i], all_ref[:, cut], preferred_element_type=F32)
            at = 0
            for ref in out_refs:
                ref[:, cut] = total[at : at + ref.shape[0]].astype(ref.dtype)
                at += ref.shape[0]

    shapes = tuple(pltpu.VMEM((keep * len(parts), 3 * hidden), dt) for dt, parts in wanted)
    scratch = [
        pltpu.VMEM((2, keep * len(groups), 2 * both), BF16),
        pltpu.VMEM((2 * both, 3 * hidden), BF16),
    ]
    return kernel_call(kernel, shapes, (here, *flats, act, act_twin), scratch, room=16)


def finish_weights(here, kept, come, hidden):
    rows = kept.shape[0]

    def kernel(here_ref, kept_ref, come_ref, in_ref, out_ref):
        total = (kept_ref[...] + come_ref[...].astype(F32)).astype(BF16)
        in_ref[...] = total[:, : 2 * hidden]
        out_ref[...] = total[:, 2 * hidden :]

    shapes = (
        jax.ShapeDtypeStruct((rows, 2 * hidden), BF16),
        jax.ShapeDtypeStruct((rows, hidden), BF16),
    )
    return kernel_call(kernel, shapes, (here, kept, come), room=4)


def body(tokens, cotangent, w_in, w_out, block_rows, block_gates, block_count):
    rows, hidden = w_out.shape[1:]
    pair = 2 * rows
    ring = lax.axis_size("dp_1")
    half = ring // 2
    here_x, here_z, core = (lax.axis_index(name) for name in DP)
    here = jnp.stack([here_x, here_z, 2 * core - 1, core]).astype(jnp.int32)

    shard = jnp.concatenate([w_in[0], w_out[0]], axis=1)
    far_shard = across(shard)
    a, b = [shard], [far_shard]
    for _ in range(1, half + 1):
        a.append(onward(a[-1]))
    for _ in range(1, half + 1):
        b.append(onward(b[-1]))
    s = [twin(jnp.concatenate([shard, far_shard]))]
    for _ in range(1, half):
        s.append(onward(s[-1]))
    pieces = []
    for p, chain in ((0, a), (1, b)):
        base = p * ring * pair
        every, part = slice(0, rows), slice(p * rows, (p + 1) * rows)
        for k in range(half + 1):
            pieces.append((chain[k], every, base + k * pair, False))
            if k < half:
                pieces.append((s[k], part, base + k * pair, True))
            if k > 0:
                came = twin(chain[k])
                pieces.append((came, every, base + (ring - k) * pair, True))
    for k in range(1, half):
        came = twin(s[k])
        for p in range(2):
            part = slice(p * rows, (p + 1) * rows)
            pieces.append((came, part, (p * ring + ring - k) * pair, False))

    near, near_gate, sent_gate = prepare(
        tokens, cotangent, block_rows[0], block_gates[0], block_count
    )
    far = around(near, -1)
    far_gate = around(sent_gate, -1)
    near_turned, *near_flat = turn_columns(here, near, twin(near), ring, pair)
    far_turned, *far_flat = turn_columns(here, far, twin(far), ring, pair)
    flats = (*near_flat, *far_flat)
    slab, act, near_score, far_score = hidden_values(
        here, near_turned, far_turned, (near_gate, far_gate), pieces, pair, hidden
    )
    act_twin = twin(act)
    far_values, near_values = token_values(here, act, slab, ring, pair, hidden)
    come = around(far_values, 1)
    come_score = around(far_score, 1)

    def terms(wanted):
        return weight_terms(here, flats, act, act_twin, wanted, ring, pair, hidden)

    mark = ring - half + 1
    begun, u = terms(
        [
            (BF16, [(1, half, False), (0, half, False)]),
            (BF16, [(1, mark, True), (0, mark, True)]),
        ]
    )
    begun = onward(begun)
    u = onward(u)
    wanted = [(F32, [(p, q % ring, False)]) for q in range(mark, ring + 1) for p in (1, 0)]
    wanted += [(F32, [(1, q, True), (0, q, True)]) for q in range(mark + 1, ring)]
    fresh = terms(wanted)
    f, o = begun[:rows], begun[rows:]
    for k in range(2, half + 1):
        f = onward((f.astype(F32) + fresh[2 * k - 4]).astype(BF16))
        o = onward((o.astype(F32) + fresh[2 * k - 3]).astype(BF16))
        if k < half:
            u = onward((u.astype(F32) + fresh[2 * half + k - 2]).astype(BF16))
    rest = twin(u).astype(F32)
    f = f.astype(F32) + fresh[2 * half - 2] + rest[:rows]
    o = o.astype(F32) + fresh[2 * half - 1] + rest[rows:]
    grad_in, grad_out = finish_weights(here, o, across(f.astype(BF16)), hidden)

    mixed, token_grad, gate_grad = finish_tokens(
        block_count, near_values, come, (near_score, come_score), block_rows[0]
    )
    return mixed, token_grad, gate_grad[None], grad_in[None], grad_out[None]


def solution(mesh):
    split = Mesh(
        mesh.devices.reshape(mesh.shape["expert"], 2, 8, 2), ("expert", "dp_0", "dp_1", "dp_2")
    )
    in_specs = (
        P(EXPERT_DP, None),
        P(EXPERT_DP, None),
        P("expert", DP, None),
        P("expert", DP, None),
        P(EXPERT_DP, None, None),
        P(EXPERT_DP, None, None),
        P(EXPERT_DP, None),
    )
    out_specs = (
        P(EXPERT_DP, None),
        P(EXPERT_DP, None),
        P(EXPERT_DP, None, None),
        P("expert", DP, None),
        P("expert", DP, None),
    )
    return jax.shard_map(body, mesh=split, in_specs=in_specs, out_specs=out_specs, check_vma=False)
```

```python
import jax
import jax.numpy as jnp
from jax import lax
from jax.experimental import pallas as pl
from jax.experimental.pallas import tpu as pltpu
from jax.sharding import Mesh
from jax.sharding import PartitionSpec as P

DP = ("dp_0", "dp_1", "dp_2")
EXPERT_DP = ("expert", "dp_0", "dp_1", "dp_2")
ZC = ("dp_1", "dp_2")
F32 = jnp.float32
BF16 = jnp.bfloat16


def around(value, distance):
    n = lax.axis_size("expert")
    return lax.ppermute(value, "expert", [(i, (i + distance) % n) for i in range(n)])


def onward(value):
    n = lax.axis_size("dp_1")
    route = [(z * 2 + c, (z + 1 - 2 * c) % n * 2 + c) for z in range(n) for c in range(2)]
    return lax.ppermute(value, ZC, route)


def twin(value):
    return lax.ppermute(value, "dp_2", [(0, 1), (1, 0)])


def across(value):
    return lax.ppermute(value, "dp_0", [(0, 1), (1, 0)])


def cols_dot(left, right):
    return lax.dot_general(left, right, (((1,), (1,)), ((), ())), preferred_element_type=F32)


def column_start(here, p, q, ring, pair):
    at = ((here[0] + p) % 2 * ring + (here[1] + here[2] * q + ring) % ring) * pair
    return pl.multiple_of(at, pair)


def kernel_call(kernel, out_shape, operands, scratch=(), room=12, aliases=None):
    vmem = pl.BlockSpec(memory_space=pltpu.VMEM)
    held = [pltpu.with_memory_space_constraint(x, pltpu.VMEM) for x in operands[1:]]
    return pl.pallas_call(
        kernel,
        out_shape=out_shape,
        in_specs=[pl.BlockSpec(memory_space=pltpu.SMEM)] + [vmem] * len(held),
        out_specs=tuple(vmem for _ in out_shape),
        scratch_shapes=scratch,
        input_output_aliases=aliases or {},
        compiler_params=pltpu.CompilerParams(vmem_limit_bytes=room << 20),
    )(operands[0], *held)


def named_tokens(rows_ref, counts_ref, block, stops, count):
    each = rows_ref.shape[0] // stops
    entries = rows_ref[block : block + 1, :]
    token = lax.broadcasted_iota(jnp.int32, (count, entries.shape[1]), 0)
    return (entries == token) & (block % each < counts_ref[0, block // each])


def prepare(tokens, cotangent, block_rows, block_gates, block_count):
    count, width = tokens.shape
    blocks = block_rows.shape[0]
    stops = block_count.shape[1]
    each = blocks // stops

    def kernel(counts_ref, rows_hbm, gates_hbm, tokens_ref, cot_ref, both_ref, *refs):
        *out_refs, rows_ref, gates_ref, sems = refs
        copies = [
            pltpu.make_async_copy(rows_hbm, rows_ref, sems.at[0]),
            pltpu.make_async_copy(gates_hbm, gates_ref, sems.at[1]),
            pltpu.make_async_copy(tokens_ref, both_ref.at[:count, :], sems.at[2]),
            pltpu.make_async_copy(cot_ref, both_ref.at[count:, :], sems.at[3]),
        ]
        for copy in copies:
            copy.start()
        for copy in copies[:2]:
            copy.wait()
        for stop in range(stops):
            total = jnp.zeros((count, 1), F32)
            for block in range(stop * each, (stop + 1) * each):
                named = named_tokens(rows_ref, counts_ref, block, stops, count)
                gates = jnp.where(named, gates_ref[block : block + 1, :], 0.0)
                total += jnp.sum(gates, axis=1, keepdims=True)
            out_refs[stop][...] = total
        for copy in copies[2:]:
            copy.wait()

    vmem = pl.BlockSpec(memory_space=pltpu.VMEM)
    hbm = pl.BlockSpec(memory_space=pltpu.HBM)
    shapes = (pltpu.VMEM((2 * count, width), BF16),) + (pltpu.VMEM((count, 1), F32),) * stops
    outside = (block_rows, block_gates, tokens, cotangent)
    return pl.pallas_call(
        kernel,
        out_shape=shapes,
        in_specs=[pl.BlockSpec(memory_space=pltpu.SMEM)] + [hbm] * 4,
        out_specs=tuple(vmem for _ in shapes),
        scratch_shapes=[
            pltpu.VMEM(block_rows.shape, jnp.int32),
            pltpu.VMEM(block_gates.shape, F32),
            pltpu.SemaphoreType.DMA((4,)),
        ],
        compiler_params=pltpu.CompilerParams(vmem_limit_bytes=4 << 20),
    )(block_count, *(pltpu.with_memory_space_constraint(x, pltpu.HBM) for x in outside))


def turn_columns(here, mine, other, ring, pair):
    both, width = mine.shape
    count = both // 2

    def kernel(here_ref, mine_ref, other_ref, turned_ref, *flat_refs):
        spot = [here_ref[i] for i in range(3)]
        for p in range(2):
            for q in range(ring):
                at = column_start(spot, p, q, ring, pair)
                to = (p * ring + q) * pair
                own = mine_ref[:, pl.ds(at, pair)]
                turned_ref[:, to : to + pair] = own
                if q >= ring // 2 or q == 0:
                    twins = other_ref[:, pl.ds(at, pair)]
                    for i in range(2):
                        rows = slice(i * count, (i + 1) * count)
                        flat_refs[i][to : to + pair, :count] = own[rows].T
                        flat_refs[i][to : to + pair, count:] = twins[rows].T

    shapes = (
        pltpu.VMEM((both, width), BF16),
        pltpu.VMEM((width, both), BF16),
        pltpu.VMEM((width, both), BF16),
    )
    return kernel_call(kernel, shapes, (here, mine, other))


class Slab:
    def __init__(self, pair):
        self.keep, self.arrays, self.plan = pair // 2, [], []

    def add(self, array, places):
        for i in range(len(places)):
            take = slice(i * self.keep, (i + 1) * self.keep)
            self.plan.append((len(self.arrays), take, *places[i]))
        self.arrays.append(array)

    def store(self, core, piece_refs, slab_ref):
        for which, take, to, twins in self.plan:
            at = to + self.keep * (1 - core if twins else core)
            rows = pl.ds(pl.multiple_of(at, self.keep), self.keep)
            slab_ref[rows, :] = piece_refs[which][take, :]


def early_slab(here, early, height):
    def kernel(here_ref, *refs):
        early.store(here_ref[3], refs[:-1], refs[-1])

    shapes = (pltpu.VMEM((height, early.arrays[0].shape[1]), BF16),)
    return kernel_call(kernel, shapes, (here, *early.arrays), room=4)[0]


def hidden_values(here, near, far, gates, slab, late, hidden):
    both, width = near.shape
    count = both // 2

    def kernel(here_ref, _, near_ref, far_ref, near_gate_ref, far_gate_ref, *refs):
        piece_refs = refs[: len(late.arrays)]
        slab_ref, act_ref, near_score_ref, far_score_ref, in_ref, cot_ref = refs[len(piece_refs) :]
        late.store(here_ref[3], piece_refs, slab_ref)
        in_ref[:count, :] = near_ref[:count, :]
        in_ref[count:, :] = far_ref[:count, :]
        cot_ref[:count, :] = near_ref[count:, :]
        cot_ref[count:, :] = far_ref[count:, :]
        slab_in = slab_ref[:, : 2 * hidden]
        preact = jnp.dot(in_ref[...], slab_in, preferred_element_type=F32)
        plain = jnp.dot(cot_ref[...], slab_ref[:, 2 * hidden :], preferred_element_type=F32)
        gate_pre, up_pre = preact[:, :hidden], preact[:, hidden:]
        gate = jnp.concatenate([near_gate_ref[...], far_gate_ref[...]])
        sig = jax.nn.sigmoid(gate_pre)
        activated = gate_pre * sig
        derivative = sig * (1.0 + gate_pre * (1.0 - sig))
        act = activated * up_pre
        act_grad = gate * plain
        act_ref[:, :hidden] = (act_grad * up_pre * derivative).astype(BF16)
        act_ref[:, hidden : 2 * hidden] = (act_grad * activated).astype(BF16)
        act_ref[:, 2 * hidden :] = (gate * act).astype(BF16)
        score = jnp.sum(act * plain, axis=1, keepdims=True)
        near_score_ref[...] = score[:count]
        far_score_ref[...] = score[count:]

    shapes = (
        pltpu.VMEM((width, 3 * hidden), BF16),
        pltpu.VMEM((both, 3 * hidden), BF16),
        pltpu.VMEM((count, 1), F32),
        pltpu.VMEM((count, 1), F32),
    )
    scratch = [pltpu.VMEM((both, width), BF16)] * 2
    operands = (here, slab, near, far, *gates, *late.arrays)
    return kernel_call(kernel, shapes, operands, scratch, aliases={1: 0})


def token_values(here, act, slab, ring, pair, hidden):
    width = slab.shape[0]
    count = act.shape[0] // 2

    def kernel(here_ref, act_ref, slab_ref, far_ref, near_ref):
        spot = [here_ref[i] for i in range(3)]
        values = (
            cols_dot(act_ref[:, 2 * hidden :], slab_ref[:, 2 * hidden :]),
            cols_dot(act_ref[:, : 2 * hidden], slab_ref[:, : 2 * hidden]),
        )
        for p in range(2):
            for q in range(ring):
                at = column_start(spot, p, q, ring, pair)
                came = (p * ring + q) * pair
                for i in range(2):
                    rows = slice(i * count, (i + 1) * count)
                    piece = values[i][:, came : came + pair]
                    near_ref[rows, pl.ds(at, pair)] = piece[:count]
                    far_ref[rows, pl.ds(at, pair)] = piece[count:].astype(BF16)

    shapes = (pltpu.VMEM((2 * count, width), BF16), pltpu.VMEM((2 * count, width), F32))
    return kernel_call(kernel, shapes, (here, act, slab))


def finish_tokens(block_count, near, come, scores, block_rows):
    both, width = near.shape
    count = both // 2
    stops = block_count.shape[1]
    each = block_rows.shape[0] // stops

    def kernel(counts_ref, near_ref, come_ref, *refs):
        score_refs, (rows_ref, mixed_ref, grad_ref, gates_ref) = refs[:stops], refs[stops:]
        mixed_ref[...] = (near_ref[:count, :] + come_ref[:count, :].astype(F32)).astype(BF16)
        grad_ref[...] = (near_ref[count:, :] + come_ref[count:, :].astype(F32)).astype(BF16)
        for block in range(stops * each):
            named = named_tokens(rows_ref, counts_ref, block, stops, count)
            picked = jnp.where(named, score_refs[block // each][...], 0.0)
            gates_ref[block : block + 1, :] = jnp.sum(picked, axis=0, keepdims=True)

    shape = jax.ShapeDtypeStruct((count, width), BF16)
    shapes = (shape, shape, jax.ShapeDtypeStruct(block_rows.shape, F32))
    return kernel_call(kernel, shapes, (block_count, near, come, *scores, block_rows))


def all_acts(act_ref, twin_ref, all_ref):
    count = act_ref.shape[0] // 2
    for i in range(2):
        rows = slice(i * count, (i + 1) * count)
        all_ref[2 * i * count : (2 * i + 1) * count, :] = act_ref[rows, :]
        all_ref[(2 * i + 1) * count : (2 * i + 2) * count, :] = twin_ref[rows, :]


def weight_terms(here, flats, act, act_twin, wanted, ring, pair, hidden):
    keep = pair // 2
    both = act.shape[0]
    groups = [group for _, parts in wanted for group in parts]

    def kernel(here_ref, *refs):
        flat_refs, (act_ref, twin_ref), out_refs = refs[:4], refs[4:6], refs[6:-2]
        left_ref, all_ref = refs[-2:]
        all_acts(act_ref, twin_ref, all_ref)
        core = here_ref[3]
        for i, cut in ((0, slice(0, 2 * hidden)), (1, slice(2 * hidden, 3 * hidden))):
            for g, (p, q, twins) in enumerate(groups):
                at = (p * ring + q) * pair + keep * (1 - core if twins else core)
                rows = pl.ds(pl.multiple_of(at, keep), keep)
                for j in range(2):
                    left_ref[i, g * keep : (g + 1) * keep, j * both : (j + 1) * both] = flat_refs[
                        2 * j + i
                    ][rows, :]
            total = jnp.dot(left_ref[i], all_ref[:, cut], preferred_element_type=F32)
            at = 0
            for ref in out_refs:
                ref[:, cut] = total[at : at + ref.shape[0]].astype(ref.dtype)
                at += ref.shape[0]

    shapes = tuple(pltpu.VMEM((keep * len(parts), 3 * hidden), dt) for dt, parts in wanted)
    scratch = [
        pltpu.VMEM((2, keep * len(groups), 2 * both), BF16),
        pltpu.VMEM((2 * both, 3 * hidden), BF16),
    ]
    return kernel_call(kernel, shapes, (here, *flats, act, act_twin), scratch, room=16)


def finish_weights(here, kept, come, hidden):
    rows = kept.shape[0]

    def kernel(here_ref, kept_ref, come_ref, in_ref, out_ref):
        total = (kept_ref[...] + come_ref[...].astype(F32)).astype(BF16)
        in_ref[...] = total[:, : 2 * hidden]
        out_ref[...] = total[:, 2 * hidden :]

    shapes = (
        jax.ShapeDtypeStruct((rows, 2 * hidden), BF16),
        jax.ShapeDtypeStruct((rows, hidden), BF16),
    )
    return kernel_call(kernel, shapes, (here, kept, come), room=4)


def body(tokens, cotangent, w_in, w_out, block_rows, block_gates, block_count):
    rows, hidden = w_out.shape[1:]
    pair = 2 * rows
    ring = lax.axis_size("dp_1")
    half = ring // 2
    here_x, here_z, core = (lax.axis_index(name) for name in DP)
    here = jnp.stack([here_x, here_z, 2 * core - 1, core]).astype(jnp.int32)

    shard = jnp.concatenate([w_in[0], w_out[0]], axis=1)
    far_shard = across(shard)
    a = [jnp.concatenate([shard, twin(shard)])]
    b, c = [far_shard], [twin(far_shard)]
    early, late = Slab(pair), Slab(pair)
    early.add(a[0], [(0, False), (0, True)])
    early.add(b[0], [(ring * pair, False)])
    early.add(c[0], [(ring * pair, True)])
    for k in range(1, half + 1):
        slab = early if k < half - 1 else late
        mine, other = k * pair, (ring - k) * pair
        mine_far, other_far = mine + ring * pair, other + ring * pair
        last = k == half
        a.append(onward(a[-1][:rows] if last else a[-1]))
        slab.add(a[k], [(mine, False)] if last else [(mine, False), (mine, True)])
        slab.add(twin(a[k]), [(other, True)] if last else [(other, True), (other, False)])
        b.append(onward(b[-1]))
        slab.add(b[k], [(mine_far, False)])
        slab.add(twin(b[k]), [(other_far, True)])
        if not last:
            c.append(onward(c[-1]))
            slab.add(c[k], [(mine_far, True)])
            slab.add(twin(c[k]), [(other_far, False)])

    near, near_gate, sent_gate = prepare(
        tokens, cotangent, block_rows[0], block_gates[0], block_count
    )
    far = around(near, -1)
    far_gate = around(sent_gate, -1)
    near_turned, *near_flat = turn_columns(here, near, twin(near), ring, pair)
    far_turned, *far_flat = turn_columns(here, far, twin(far), ring, pair)
    flats = (*near_flat, *far_flat)
    slab, act, near_score, far_score = hidden_values(
        here,
        near_turned,
        far_turned,
        (near_gate, far_gate),
        early_slab(here, early, near.shape[1]),
        late,
        hidden,
    )
    act_twin = twin(act)
    far_values, near_values = token_values(here, act, slab, ring, pair, hidden)
    come = around(far_values, 1)
    come_score = around(far_score, 1)

    def terms(wanted):
        return weight_terms(here, flats, act, act_twin, wanted, ring, pair, hidden)

    mark = ring - half + 1
    begun, u = terms(
        [
            (BF16, [(1, half, False), (0, half, False)]),
            (BF16, [(1, mark, True), (0, mark, True)]),
        ]
    )
    begun = onward(begun)
    u = onward(u)
    wanted = [(F32, [(p, q % ring, False)]) for q in range(mark, ring + 1) for p in (1, 0)]
    wanted += [(F32, [(1, q, True), (0, q, True)]) for q in range(mark + 1, ring)]
    fresh = terms(wanted)
    f, o = begun[:rows], begun[rows:]
    for k in range(2, half + 1):
        f = onward((f.astype(F32) + fresh[2 * k - 4]).astype(BF16))
        o = onward((o.astype(F32) + fresh[2 * k - 3]).astype(BF16))
        if k < half:
            u = onward((u.astype(F32) + fresh[2 * half + k - 2]).astype(BF16))
    rest = twin(u).astype(F32)
    f = f.astype(F32) + fresh[2 * half - 2] + rest[:rows]
    o = o.astype(F32) + fresh[2 * half - 1] + rest[rows:]
    grad_in, grad_out = finish_weights(here, o, across(f.astype(BF16)), hidden)

    mixed, token_grad, gate_grad = finish_tokens(
        block_count, near_values, come, (near_score, come_score), block_rows[0]
    )
    return mixed, token_grad, gate_grad[None], grad_in[None], grad_out[None]


def solution(mesh):
    split = Mesh(
        mesh.devices.reshape(mesh.shape["expert"], 2, 8, 2), ("expert", "dp_0", "dp_1", "dp_2")
    )
    in_specs = (
        P(EXPERT_DP, None),
        P(EXPERT_DP, None),
        P("expert", DP, None),
        P("expert", DP, None),
        P(EXPERT_DP, None, None),
        P(EXPERT_DP, None, None),
        P(EXPERT_DP, None),
    )
    out_specs = (
        P(EXPERT_DP, None),
        P(EXPERT_DP, None),
        P(EXPERT_DP, None, None),
        P("expert", DP, None),
        P("expert", DP, None),
    )
    return jax.shard_map(body, mesh=split, in_specs=in_specs, out_specs=out_specs, check_vma=False)
```
